32 devices in a mesh: grp: 2 (over x), ex: 8 (over z, y), lay: 2 (over core).
Axes of the slice: x: 2, y: 2, z: 4, core: 2. Of those that a mesh axis runs over, the one named last changes fastest.
Arguments:
- queries: bfloat16 [512, 2, 4096], P('ex', 'lay'), may hold values from -4 to 4
- basis_s: float32 [2, 64, 64], P('lay'), may hold values from -1 to 1, as said below
- basis_a: float32 [2, 64, 64], P('lay'), may hold values from -1 to 1, as said below
- eigvals: float32 [2, 64, 64], P('lay'), may hold values from 0.004 to 20, as said below
- train_grads: bfloat16 [16384, 2, 4096], P(('grp', 'ex'), 'lay'), parts along dimension 0, may hold values from -0.0625 to 0.0625
- example_ids: int32 [16, 1024], P(('grp', 'ex')), parts along dimension 0, may hold values from 0 to 1023, each once within a row
Outputs:
- scores: float32 [512, 16384], P(None, ('grp', 'ex', 'lay')), parts along dimension 1
The draws below stay inside these ranges and needn't reach their ends.
There are 2 independent parts, one for each index of `grp`. The reference program is written for one: setup_inputs(seed, part) draws one part's arguments, and reference() takes and returns one part's arrays. A program takes and returns all parts, laid end to end along the dimension named above; an argument that names none is the same for every part. Nothing has to cross between parts.
Inputs may be any that keep to these rules, and one draw needn't show every extreme that they name: `basis_s`: each layer's basis has orthonormal columns. `basis_a`: each layer's basis has orthonormal columns. `eigvals`: positive.
All inputs are finite; a program needn't handle non-finite values.
Results may differ from the reference program's by a relative error of at most 0.0029.
Values may be sent and summed in bfloat16 or wider, within the bound.
A program may use at most 64 MiB of HBM per device.

```python
import math
import jax
import jax.numpy as jnp
from jax import lax

R = 64
F = 4096
LAYERS = 2
Q = 512
EXD = 1024
EXAMPLES = 8192
N_EX = 8


def cosine_basis(key):

    def one_layer(layer_key):
        key_rows, key_cols, key_signs = jax.random.split(layer_key, 3)
        row_perm = jax.random.permutation(key_rows, R).astype(jnp.float32)
        col_perm = jax.random.permutation(key_cols, R).astype(jnp.float32)
        signs = (jax.random.randint(key_signs, (R,), 0, 2) * 2 - 1).astype(jnp.float32)
        angles = math.pi * (row_perm[:, None] + 0.5) * col_perm[None, :] / R
        norms = jnp.where(col_perm[None, :] == 0.0, math.sqrt(1.0 / R), math.sqrt(2.0 / R))
        return jnp.cos(angles) * norms * signs[None, :]
    return jax.vmap(one_layer)(jax.random.split(key, LAYERS))


def draw_basis_s(key, part):
    return cosine_basis(jax.random.fold_in(key, 11))


def draw_basis_a(key, part):
    return cosine_basis(jax.random.fold_in(key, 23))


def draw_eigvals(key, part):
    own_key = jax.random.fold_in(key, 37)
    key_one = jax.random.fold_in(own_key, 0)
    return jnp.exp(jax.random.uniform(key_one, (LAYERS, R, R), jnp.float32, math.log(0.05), math.log(20.0)))


def block_levels(key, shape, cuts, low, high):
    level, own = 1.0, jax.random.fold_in(key, 6)
    for dim, shards_of in cuts:
        steps = jnp.exp(jax.random.uniform(jax.random.fold_in(own, dim), (shards_of,), jnp.float32, low / len(cuts), high / len(cuts)))
        level = level * jnp.repeat(steps, shape[dim] // shards_of).reshape([-1 if axis == dim else 1 for axis in range(len(shape))])
    return level


def bell_draw(key, shape, deviation, most, cuts=(), kind=jnp.bfloat16):
    gain = block_levels(key, shape, cuts, -0.22, 0.18) if cuts else 1.0
    result = jax.random.normal(key, shape, jnp.float32) * deviation * gain
    return jnp.minimum(jnp.maximum(result, -most), most).astype(kind)


def setup_inputs(seed: int = 0, part: int = 0) -> dict:
    keys = jax.random.split(jax.random.key(seed), 7)
    part_keys = jax.random.split(jax.random.fold_in(keys[6], part), 7)
    queries = bell_draw(keys[0], (Q, LAYERS, F), 0.5, 4.0, ((0, 8), (1, 2)))
    basis_s = draw_basis_s(jax.random.fold_in(keys[6], 71), part)
    basis_a = draw_basis_a(jax.random.fold_in(keys[6], 71), part)
    eigvals = draw_eigvals(jax.random.fold_in(keys[6], 71), part)
    train_grads = bell_draw(part_keys[4], (EXAMPLES, LAYERS, F), (LAYERS * F) ** -0.5, 0.0625, ((0, 8), (1, 2)))
    example_ids = jax.vmap(lambda own: jax.random.permutation(own, EXD))(jax.random.split(part_keys[5], N_EX)).reshape((N_EX, EXD)).astype(jnp.int32)
    return {"queries": queries, "basis_s": basis_s, "basis_a": basis_a, "eigvals": eigvals, "train_grads": train_grads, "example_ids": example_ids}


damp_ratio = 0.1


def precondition(grads, basis_s, basis_a, eigvals):
    number_rows = grads.shape[0]
    layer_count = grads.shape[1]
    rank = basis_s.shape[-1]
    highest = lax.Precision.HIGHEST
    expanded = grads.astype(jnp.float32).reshape(number_rows, layer_count, rank, rank)
    half_turn = jnp.einsum('nlik,lkm->nlim', expanded, basis_a, precision=highest)
    rotated = jnp.einsum('lij,nlim->nljm', basis_s, half_turn, precision=highest)
    damping = damp_ratio * jnp.mean(eigvals, axis=(1, 2), keepdims=True)
    scaled = rotated / (eigvals + damping)[None]
    turned_back = jnp.einsum('nljm,lpm->nljp', scaled, basis_a, precision=highest)
    restored = jnp.einsum('lij,nljp->nlip', basis_s, turned_back, precision=highest)
    return restored.reshape(number_rows, layer_count, rank * rank).astype(jnp.bfloat16)


def reference(queries, basis_s, basis_a, eigvals, train_grads, example_ids):
    conditioned = precondition(queries, basis_s, basis_a, eigvals)
    summed = jnp.zeros((Q, EXAMPLES), jnp.float32)
    for layer in range(LAYERS):
        summed = summed + jnp.dot(conditioned[:, layer], train_grads[:, layer].T, preferred_element_type=jnp.float32)
    block_rows = (jnp.arange(N_EX, dtype=jnp.int32)[:, None] * EXD + example_ids.astype(jnp.int32)).reshape(-1)
    return jnp.take(summed, block_rows, axis=1)
```

```python
import functools

import jax
import jax.numpy as jnp
from jax import lax
from jax.experimental import pallas as pl
from jax.experimental.pallas import tpu as pltpu
from jax.sharding import PartitionSpec as P

damp_ratio = 0.1
pairs = 4
MESH = pl.DeviceIdType.MESH


def precondition(grads, basis_s, basis_a, eigvals):
    number_rows = grads.shape[0]
    layer_count = grads.shape[1]
    rank = basis_s.shape[-1]
    highest = lax.Precision.HIGHEST
    expanded = grads.astype(jnp.float32).reshape(number_rows, layer_count, rank, rank)
    half_turn = jnp.einsum("nlik,lkm->nlim", expanded, basis_a, precision=highest)
    rotated = jnp.einsum("lij,nlim->nljm", basis_s, half_turn, precision=highest)
    damping = damp_ratio * jnp.mean(eigvals, axis=(1, 2), keepdims=True)
    scaled = rotated / (eigvals + damping)[None]
    turned_back = jnp.einsum("nljm,lpm->nljp", scaled, basis_a, precision=highest)
    restored = jnp.einsum("lij,nljp->nlip", basis_s, turned_back, precision=highest)
    return restored.reshape(number_rows, layer_count, rank * rank).astype(jnp.bfloat16)


def score_kernel(
    line, own_ref, ids_ref, train_ref, out_ref,
    stored, hot, perm, held, acc, arrived,
    load_sem, own_sem, z_recv, zr_send, zl_send, y_recv, y_send, x_recv, x_send, c_recv, c_send,
):
    grp = lax.axis_index("grp")
    ex = lax.axis_index("ex")
    core = lax.axis_index("lay")
    zz = ex // 2
    w = ex % 2
    side = grp % 2
    rows = own_ref.shape[2]
    examples = train_ref.shape[0]
    chunk = own_ref.shape[3]
    half = examples // 2
    right = {"ex": lax.rem(ex + 2, 2 * line)}
    left = {"ex": lax.rem(ex + 2 * line - 2, 2 * line)}
    across_y = {"ex": zz * 2 + (1 - w)}
    across_x = {"grp": (grp // 2) * 2 + (1 - side)}
    across_c = {"lay": 1 - core}
    has_left = zz > 0
    has_right = zz < line - 1

    def load(p):
        return pltpu.make_async_copy(
            train_ref.at[:, pl.ds(p * 2 * chunk, 2 * chunk)], stored.at[p], load_sem.at[p]
        )

    def z_copy(src, b, p, send, target):
        return pltpu.make_async_remote_copy(
            src_ref=src, dst_ref=held.at[b, p, :, w], send_sem=send.at[b, p],
            recv_sem=z_recv.at[b, p], device_id=target, device_id_type=MESH,
        )

    def own_z(p, send, target):
        return z_copy(own_ref.at[p], zz, p, send, target)

    def pass_z(b, p, send, target):
        return z_copy(held.at[b, p, :, w], b, p, send, target)

    def y_copy(src, b, p):
        return pltpu.make_async_remote_copy(
            src_ref=src, dst_ref=held.at[b, p, side, w], send_sem=y_send.at[b, p],
            recv_sem=y_recv.at[b, p], device_id=across_y, device_id_type=MESH,
        )

    def y_arrival(b, p):
        slot = held.at[b, p, side, 1 - w]
        return pltpu.make_async_remote_copy(
            src_ref=slot, dst_ref=slot, send_sem=y_send.at[b, p],
            recv_sem=y_recv.at[b, p], device_id=across_y, device_id_type=MESH,
        )

    def x_copy(b, p, which):
        slot = held.at[b, p, which, 1 - w]
        return pltpu.make_async_remote_copy(
            src_ref=slot, dst_ref=slot, send_sem=x_send.at[b, p],
            recv_sem=x_recv.at[b, p], device_id=across_x, device_id_type=MESH,
        )

    def c_copy(b):
        return pltpu.make_async_remote_copy(
            src_ref=acc.at[b, 1 - core], dst_ref=arrived.at[b], send_sem=c_send.at[b],
            recv_sem=c_recv.at[b], device_id=across_c, device_id_type=MESH,
        )

    @pl.loop(0, pairs)
    def _(p):
        load(p).start()

    barrier = pltpu.get_barrier_semaphore()

    @pl.when(has_left)
    def _():
        pl.semaphore_signal(barrier, inc=1, device_id=left, device_id_type=MESH)

    @pl.when(has_right)
    def _():
        pl.semaphore_signal(barrier, inc=1, device_id=right, device_id_type=MESH)

    for target in (across_y, across_x, across_c):
        pl.semaphore_signal(barrier, inc=1, device_id=target, device_id_type=MESH)
    pl.semaphore_wait(barrier, 3 + has_left.astype(jnp.int32) + has_right.astype(jnp.int32))

    @pl.loop(0, pairs)
    def _(p):
        @pl.when(has_right)
        def _():
            own_z(p, zr_send, right).start()

        @pl.when(has_left)
        def _():
            own_z(p, zl_send, left).start()

        y_copy(own_ref.at[p, side], zz, p).start()

    @pl.loop(0, pairs)
    def _(p):
        pltpu.make_async_copy(own_ref.at[p], held.at[zz, p, :, w], own_sem.at[p]).start()

    spread = jnp.broadcast_to(ids_ref[...].astype(jnp.float32), (128, examples)).T
    lanes = lax.broadcasted_iota(jnp.int32, (examples, 128), 1).astype(jnp.float32)
    for tile in range(examples // 128):
        hot[:, tile * 128:(tile + 1) * 128] = jnp.where(
            spread == lanes + float(tile * 128), 1.0, 0.0
        ).astype(jnp.bfloat16)

    @pl.loop(0, pairs)
    def _(p):
        pltpu.make_async_copy(own_ref.at[p], held.at[zz, p, :, w], own_sem.at[p]).wait()

    def both(s, act):
        t = s // pairs
        p = s % pairs
        valid = jnp.logical_and(s >= 0, t < line)

        @pl.when(jnp.logical_and(valid, zz - t >= 0))
        def _():
            act(zz - t, t, p, True)

        @pl.when(jnp.logical_and(jnp.logical_and(valid, t > 0), zz + t < line))
        def _():
            act(zz + t, t, p, False)

    def relay_z(b, t, p, from_left):
        @pl.when(t > 0)
        def _():
            if from_left:
                pass_z(b, p, zr_send, left).wait_recv()

                @pl.when(has_right)
                def _():
                    pass_z(b, p, zr_send, right).start()
            else:
                pass_z(b, p, zl_send, right).wait_recv()

                @pl.when(has_left)
                def _():
                    pass_z(b, p, zl_send, left).start()

            y_copy(held.at[b, p, side, w], b, p).start()

    def relay_x(b, t, p, from_left):
        y_arrival(b, p).wait_recv()
        x_copy(b, p, side).start()

    def multiply(b, t, p, from_left):
        x_copy(b, p, 1 - side).wait_recv()
        for part in range(2):
            value = None
            for h in range(2):
                term = lax.dot_general(
                    held[b, p, h].reshape(2 * rows, chunk),
                    perm[p, h, part * half:(part + 1) * half, :],
                    (((1,), (1,)), ((), ())), preferred_element_type=jnp.float32,
                )
                value = term if value is None else value + term

            @pl.when(p == 0)
            def _():
                acc[b, part] = value

            @pl.when(p > 0)
            def _():
                acc[b, part] = acc[b, part] + value

        @pl.when(p == pairs - 1)
        def _():
            c_copy(b).start()

    def finish(b, t, p, from_left):
        @pl.when(p == pairs - 1)
        def _():
            c_copy(b).wait_recv()
            out_ref[b] = acc[b, core] + arrived[b]

    @pl.loop(0, line * pairs + 3)
    def _(s):
        both(s, relay_z)
        both(s - 1, relay_x)

        @pl.when(s < pairs)
        def _():
            load(s).wait()

            @pl.loop(0, 4)
            def _(part):
                quarter = examples // 4
                picked = pl.ds(part * quarter, quarter)
                for h in range(2):
                    perm[s, h, picked, :] = jnp.dot(
                        hot[picked, :], stored[s, :, h * chunk:(h + 1) * chunk],
                        preferred_element_type=jnp.float32,
                    ).astype(jnp.bfloat16)

        both(s - 2, multiply)
        both(s - 3, finish)

    @pl.loop(0, line * pairs)
    def _(s):
        b = s // pairs
        p = s % pairs

        @pl.when(jnp.logical_and(has_right, b <= zz))
        def _():
            pass_z(b, p, zr_send, right).wait_send()

        @pl.when(jnp.logical_and(has_left, b >= zz))
        def _():
            pass_z(b, p, zl_send, left).wait_send()

        y_copy(held.at[b, p, side, w], b, p).wait_send()
        x_copy(b, p, side).wait_send()

        @pl.when(p == 0)
        def _():
            c_copy(b).wait_send()


def scores_of(own, ids, train, devices):
    rows = own.shape[2]
    chunk = own.shape[3]
    examples = train.shape[0]
    line = devices // 2
    dma = pltpu.SemaphoreType.DMA
    grid_sems = [dma((line, pairs)) for _ in range(7)]
    return pl.pallas_call(
        functools.partial(score_kernel, line),
        out_shape=jax.ShapeDtypeStruct((line, 2 * rows, examples // 2), jnp.float32),
        in_specs=[
            pl.BlockSpec(memory_space=pltpu.VMEM),
            pl.BlockSpec(memory_space=pltpu.VMEM),
            pl.BlockSpec(memory_space=pl.ANY),
        ],
        out_specs=pl.BlockSpec(memory_space=pltpu.VMEM),
        scratch_shapes=[
            pltpu.VMEM((pairs, examples, 2 * chunk), jnp.bfloat16),
            pltpu.VMEM((examples, examples), jnp.bfloat16),
            pltpu.VMEM((pairs, 2, examples, chunk), jnp.bfloat16),
            pltpu.VMEM((line, pairs, 2, 2, rows, chunk), jnp.bfloat16),
            pltpu.VMEM((line, 2, 2 * rows, examples // 2), jnp.float32),
            pltpu.VMEM((line, 2 * rows, examples // 2), jnp.float32),
            dma((pairs,)),
            dma((pairs,)),
            *grid_sems,
            dma((line,)),
            dma((line,)),
        ],
        compiler_params=pltpu.CompilerParams(
            collective_id=0, has_side_effects=True, vmem_limit_bytes=56 * 1024 * 1024
        ),
    )(own, ids, train)


def shards(devices, queries, basis_s, basis_a, eigvals, train_grads, example_ids):
    stored = train_grads.reshape(train_grads.shape[0], -1)
    own_rows = precondition(queries, basis_s, basis_a, eigvals)
    rows = own_rows.shape[0]
    cut = own_rows.reshape(rows, 2 * pairs, -1).transpose(1, 0, 2)
    cut = cut.reshape(pairs, 2, rows, cut.shape[-1])
    scores = scores_of(cut, example_ids, stored, devices)
    return scores.reshape(devices * rows, -1)


def solution(mesh):
    return jax.shard_map(
        functools.partial(shards, mesh.shape["ex"]),
        mesh=mesh,
        in_specs=(
            P("ex", "lay", None),
            P("lay", None, None),
            P("lay", None, None),
            P("lay", None, None),
            P(("grp", "ex"), "lay", None),
            P(("grp", "ex"), None),
        ),
        out_specs=P(None, ("grp", "ex", "lay")),
        check_vma=False,
    )
```

```python
import functools

import jax
import jax.numpy as jnp
from jax import lax
from jax.experimental import pallas as pl
from jax.experimental.pallas import tpu as pltpu
from jax.sharding import PartitionSpec as P

damp_ratio = 0.1
pairs = 4
MESH = pl.DeviceIdType.MESH


def precondition(grads, basis_s, basis_a, eigvals):
    number_rows = grads.shape[0]
    layer_count = grads.shape[1]
    rank = basis_s.shape[-1]
    highest = lax.Precision.HIGHEST
    expanded = grads.astype(jnp.float32).reshape(number_rows, layer_count, rank, rank)
    half_turn = jnp.einsum("nlik,lkm->nlim", expanded, basis_a, precision=highest)
    rotated = jnp.einsum("lij,nlim->nljm", basis_s, half_turn, precision=highest)
    damping = damp_ratio * jnp.mean(eigvals, axis=(1, 2), keepdims=True)
    scaled = rotated / (eigvals + damping)[None]
    turned_back = jnp.einsum("nljm,lpm->nljp", scaled, basis_a, precision=highest)
    restored = jnp.einsum("lij,nljp->nlip", basis_s, turned_back, precision=highest)
    return restored.reshape(number_rows, layer_count, rank * rank).astype(jnp.bfloat16)


def score_kernel(
    line, own_ref, ids_ref, train_ref, out_ref,
    stored, hot, perm, held, acc, arrived,
    load_sem, own_sem, z_recv, zr_send, zl_send, y_recv, y_send, x_recv, x_send, c_recv, c_send,
):
    grp = lax.axis_index("grp")
    ex = lax.axis_index("ex")
    core = lax.axis_index("lay")
    zz = ex // 2
    w = ex % 2
    side = grp % 2
    rows = own_ref.shape[2]
    examples = train_ref.shape[0]
    chunk = own_ref.shape[3]
    half = examples // 2
    right = {"ex": lax.rem(ex + 2, 2 * line)}
    left = {"ex": lax.rem(ex + 2 * line - 2, 2 * line)}
    across_y = {"ex": zz * 2 + (1 - w)}
    across_x = {"grp": (grp // 2) * 2 + (1 - side)}
    across_c = {"lay": 1 - core}
    has_left = zz > 0
    has_right = zz < line - 1

    def load(p):
        return pltpu.make_async_copy(
            train_ref.at[:, pl.ds(p * 2 * chunk, 2 * chunk)], stored.at[p], load_sem.at[p]
        )

    def z_copy(src, b, p, send, target):
        return pltpu.make_async_remote_copy(
            src_ref=src, dst_ref=held.at[b, p, :, w], send_sem=send.at[b, p],
            recv_sem=z_recv.at[b, p], device_id=target, device_id_type=MESH,
        )

    def own_z(p, send, target):
        return z_copy(own_ref.at[p], zz, p, send, target)

    def pass_z(b, p, send, target):
        return z_copy(held.at[b, p, :, w], b, p, send, target)

    def y_copy(src, b, p):
        return pltpu.make_async_remote_copy(
            src_ref=src, dst_ref=held.at[b, p, side, w], send_sem=y_send.at[b, p],
            recv_sem=y_recv.at[b, p], device_id=across_y, device_id_type=MESH,
        )

    def y_arrival(b, p):
        slot = held.at[b, p, side, 1 - w]
        return pltpu.make_async_remote_copy(
            src_ref=slot, dst_ref=slot, send_sem=y_send.at[b, p],
            recv_sem=y_recv.at[b, p], device_id=across_y, device_id_type=MESH,
        )

    def x_copy(b, p, which):
        slot = held.at[b, p, which, 1 - w]
        return pltpu.make_async_remote_copy(
            src_ref=slot, dst_ref=slot, send_sem=x_send.at[b, p],
            recv_sem=x_recv.at[b, p], device_id=across_x, device_id_type=MESH,
        )

    def c_copy(b):
        return pltpu.make_async_remote_copy(
            src_ref=acc.at[b, 1 - core], dst_ref=arrived.at[b], send_sem=c_send.at[b],
            recv_sem=c_recv.at[b], device_id=across_c, device_id_type=MESH,
        )

    @pl.loop(0, pairs)
    def _(p):
        load(p).start()

    barrier = pltpu.get_barrier_semaphore()

    @pl.when(has_left)
    def _():
        pl.semaphore_signal(barrier, inc=1, device_id=left, device_id_type=MESH)

    @pl.when(has_right)
    def _():
        pl.semaphore_signal(barrier, inc=1, device_id=right, device_id_type=MESH)

    for target in (across_y, across_x, across_c):
        pl.semaphore_signal(barrier, inc=1, device_id=target, device_id_type=MESH)
    pl.semaphore_wait(barrier, 3 + has_left.astype(jnp.int32) + has_right.astype(jnp.int32))

    @pl.loop(0, pairs)
    def _(p):
        @pl.when(has_right)
        def _():
            own_z(p, zr_send, right).start()

        @pl.when(has_left)
        def _():
            own_z(p, zl_send, left).start()

        y_copy(own_ref.at[p, side], zz, p).start()

    @pl.loop(0, pairs)
    def _(p):
        pltpu.make_async_copy(own_ref.at[p], held.at[zz, p, :, w], own_sem.at[p]).start()

    spread = jnp.broadcast_to(ids_ref[...].astype(jnp.float32), (128, examples)).T
    lanes = lax.broadcasted_iota(jnp.int32, (examples, 128), 1).astype(jnp.float32)
    for tile in range(examples // 128):
        hot[:, tile * 128:(tile + 1) * 128] = jnp.where(
            spread == lanes + float(tile * 128), 1.0, 0.0
        ).astype(jnp.bfloat16)

    @pl.loop(0, pairs)
    def _(p):
        pltpu.make_async_copy(own_ref.at[p], held.at[zz, p, :, w], own_sem.at[p]).wait()

    def both(s, act):
        t = s // pairs
        p = s % pairs
        valid = jnp.logical_and(jnp.asarray(s) >= 0, jnp.asarray(t) < line)

        @pl.when(jnp.logical_and(valid, zz - t >= 0))
        def _():
            act(zz - t, t, p, True)

        @pl.when(jnp.logical_and(jnp.logical_and(valid, jnp.asarray(t) > 0), zz + t < line))
        def _():
            act(zz + t, t, p, False)

    def relay_z(b, t, p, from_left):
        @pl.when(t > 0)
        def _():
            if from_left:
                pass_z(b, p, zr_send, left).wait_recv()

                @pl.when(has_right)
                def _():
                    pass_z(b, p, zr_send, right).start()
            else:
                pass_z(b, p, zl_send, right).wait_recv()

                @pl.when(has_left)
                def _():
                    pass_z(b, p, zl_send, left).start()

            y_copy(held.at[b, p, side, w], b, p).start()

    def relay_x(b, t, p, from_left):
        y_arrival(b, p).wait_recv()
        x_copy(b, p, side).start()

    def multiply(b, t, p, from_left):
        x_copy(b, p, 1 - side).wait_recv()
        for part in range(2):
            value = None
            for h in range(2):
                term = lax.dot_general(
                    held[b, p, h].reshape(2 * rows, chunk),
                    perm[p, h, part * half:(part + 1) * half, :],
                    (((1,), (1,)), ((), ())), preferred_element_type=jnp.float32,
                )
                value = term if value is None else value + term

            @pl.when(p == 0)
            def _():
                acc[b, part] = value

            @pl.when(p > 0)
            def _():
                acc[b, part] = acc[b, part] + value

        @pl.when(p == pairs - 1)
        def _():
            c_copy(b).start()

    def finish(b, t, p, from_left):
        @pl.when(p == pairs - 1)
        def _():
            c_copy(b).wait_recv()
            out_ref[b] = acc[b, core] + arrived[b]

    @pl.loop(0, pairs)
    def _(p):
        relay_x(zz, 0, p, True)

    def reached(s):
        ready = jnp.minimum(2 * (s - pairs + 1), s + pairs - 1)
        return jnp.minimum(jnp.maximum(ready, 0), line * pairs)

    @pl.loop(0, (line + 1) * pairs)
    def _(s):
        both(s + pairs, relay_z)

        @pl.when(s > 0)
        def _():
            both(s + pairs - 1, relay_x)

        @pl.when(s < pairs)
        def _():
            load(s).wait()

            @pl.loop(0, 4)
            def _(part):
                quarter = examples // 4
                picked = pl.ds(part * quarter, quarter)
                for h in range(2):
                    perm[s, h, picked, :] = jnp.dot(
                        hot[picked, :], stored[s, :, h * chunk:(h + 1) * chunk],
                        preferred_element_type=jnp.float32,
                    ).astype(jnp.bfloat16)

        @pl.loop(reached(s - 1), reached(s))
        def _(m):
            both(m, multiply)
            both(m - 1, finish)

    both(line * pairs - 1, finish)

    @pl.loop(0, line * pairs)
    def _(s):
        b = s // pairs
        p = s % pairs

        @pl.when(jnp.logical_and(has_right, b <= zz))
        def _():
            pass_z(b, p, zr_send, right).wait_send()

        @pl.when(jnp.logical_and(has_left, b >= zz))
        def _():
            pass_z(b, p, zl_send, left).wait_send()

        y_copy(held.at[b, p, side, w], b, p).wait_send()
        x_copy(b, p, side).wait_send()

        @pl.when(p == 0)
        def _():
            c_copy(b).wait_send()


def scores_of(own, ids, train, devices):
    rows = own.shape[2]
    chunk = own.shape[3]
    examples = train.shape[0]
    line = devices // 2
    dma = pltpu.SemaphoreType.DMA
    grid_sems = [dma((line, pairs)) for _ in range(7)]
    return pl.pallas_call(
        functools.partial(score_kernel, line),
        out_shape=jax.ShapeDtypeStruct((line, 2 * rows, examples // 2), jnp.float32),
        in_specs=[
            pl.BlockSpec(memory_space=pltpu.VMEM),
            pl.BlockSpec(memory_space=pltpu.VMEM),
            pl.BlockSpec(memory_space=pl.ANY),
        ],
        out_specs=pl.BlockSpec(memory_space=pltpu.VMEM),
        scratch_shapes=[
            pltpu.VMEM((pairs, examples, 2 * chunk), jnp.bfloat16),
            pltpu.VMEM((examples, examples), jnp.bfloat16),
            pltpu.VMEM((pairs, 2, examples, chunk), jnp.bfloat16),
            pltpu.VMEM((line, pairs, 2, 2, rows, chunk), jnp.bfloat16),
            pltpu.VMEM((line, 2, 2 * rows, examples // 2), jnp.float32),
            pltpu.VMEM((line, 2 * rows, examples // 2), jnp.float32),
            dma((pairs,)),
            dma((pairs,)),
            *grid_sems,
            dma((line,)),
            dma((line,)),
        ],
        compiler_params=pltpu.CompilerParams(
            collective_id=0, has_side_effects=True, vmem_limit_bytes=56 * 1024 * 1024
        ),
    )(own, ids, train)


def shards(devices, queries, basis_s, basis_a, eigvals, train_grads, example_ids):
    stored = train_grads.reshape(train_grads.shape[0], -1)
    own_rows = precondition(queries, basis_s, basis_a, eigvals)
    rows = own_rows.shape[0]
    cut = own_rows.reshape(rows, 2 * pairs, -1).transpose(1, 0, 2)
    cut = cut.reshape(pairs, 2, rows, cut.shape[-1])
    scores = scores_of(cut, example_ids, stored, devices)
    return scores.reshape(devices * rows, -1)


def solution(mesh):
    return jax.shard_map(
        functools.partial(shards, mesh.shape["ex"]),
        mesh=mesh,
        in_specs=(
            P("ex", "lay", None),
            P("lay", None, None),
            P("lay", None, None),
            P("lay", None, None),
            P(("grp", "ex"), "lay", None),
            P(("grp", "ex"), None),
        ),
        out_specs=P(None, ("grp", "ex", "lay")),
        check_vma=False,
    )
```

```python
import functools

import jax
import jax.numpy as jnp
from jax import lax
from jax.experimental import pallas as pl
from jax.experimental.pallas import tpu as pltpu
from jax.sharding import PartitionSpec as P

damp_ratio = 0.1
pairs = 4
shared = 2
MESH = pl.DeviceIdType.MESH


def precondition(grads, basis_s, basis_a, eigvals):
    number_rows = grads.shape[0]
    layer_count = grads.shape[1]
    rank = basis_s.shape[-1]
    highest = lax.Precision.HIGHEST
    expanded = grads.astype(jnp.float32).reshape(number_rows, layer_count, rank, rank)
    half_turn = jnp.einsum("nlik,lkm->nlim", expanded, basis_a, precision=highest)
    rotated = jnp.einsum("lij,nlim->nljm", basis_s, half_turn, precision=highest)
    damping = damp_ratio * jnp.mean(eigvals, axis=(1, 2), keepdims=True)
    scaled = rotated / (eigvals + damping)[None]
    turned_back = jnp.einsum("nljm,lpm->nljp", scaled, basis_a, precision=highest)
    restored = jnp.einsum("lij,nljp->nlip", basis_s, turned_back, precision=highest)
    return restored.reshape(number_rows, layer_count, rank * rank).astype(jnp.bfloat16)


def score_kernel(
    line, own_ref, ids_ref, train_ref, out_ref,
    stored, hot, perm, held, acc, arrived,
    load_sem, own_sem, z_recv, zr_send, zl_send, y_recv, y_send, x_recv, x_send, twin_recv, twin_send,
    c_recv, c_send,
):
    grp = lax.axis_index("grp")
    ex = lax.axis_index("ex")
    core = lax.axis_index("lay")
    zz = ex // 2
    w = ex % 2
    side = grp % 2
    rows = own_ref.shape[2]
    examples = train_ref.shape[0]
    chunk = own_ref.shape[3]
    half = examples // 2
    right = {"ex": lax.rem(ex + 2, 2 * line)}
    left = {"ex": lax.rem(ex + 2 * line - 2, 2 * line)}
    across_y = {"ex": zz * 2 + (1 - w)}
    across_x = {"grp": (grp // 2) * 2 + (1 - side)}
    across_c = {"lay": 1 - core}
    has_left = zz > 0
    has_right = zz < line - 1

    def load(p):
        return pltpu.make_async_copy(
            train_ref.at[:, pl.ds(p * 2 * chunk, 2 * chunk)], stored.at[p], load_sem.at[p]
        )

    def pick(p, first, second):
        @pl.when(p < shared)
        def _():
            first()

        @pl.when(p >= shared)
        def _():
            second()

    def z_copy(src, b, p, which, send, target):
        return pltpu.make_async_remote_copy(
            src_ref=src, dst_ref=held.at[b, p, which, w], send_sem=send.at[b, p],
            recv_sem=z_recv.at[b, p], device_id=target, device_id_type=MESH,
        )

    def own_z(p, send, target):
        pick(
            p,
            lambda: z_copy(own_ref.at[p, side], zz, p, side, send, target).start(),
            lambda: z_copy(own_ref.at[p], zz, p, slice(None), send, target).start(),
        )

    def pass_z(b, p, send, target, act):
        pick(
            p,
            lambda: act(z_copy(held.at[b, p, side, w], b, p, side, send, target)),
            lambda: act(z_copy(held.at[b, p, :, w], b, p, slice(None), send, target)),
        )

    def begin(copy):
        copy.start()

    def landed(copy):
        copy.wait_recv()

    def left_here(copy):
        copy.wait_send()

    def y_copy(src, b, p):
        return pltpu.make_async_remote_copy(
            src_ref=src, dst_ref=held.at[b, p, side, w], send_sem=y_send.at[b, p],
            recv_sem=y_recv.at[b, p], device_id=across_y, device_id_type=MESH,
        )

    def y_whole(b, p, column):
        slot = held.at[b, p, :, column]
        return pltpu.make_async_remote_copy(
            src_ref=slot, dst_ref=slot, send_sem=y_send.at[b, p],
            recv_sem=y_recv.at[b, p], device_id=across_y, device_id_type=MESH,
        )

    def twin_copy(b, p, which):
        slot = held.at[b, p, which, w]
        return pltpu.make_async_remote_copy(
            src_ref=slot, dst_ref=slot, send_sem=twin_send.at[b, p],
            recv_sem=twin_recv.at[b, p], device_id=across_x, device_id_type=MESH,
        )

    def whole_over_y(t, p):
        return jnp.logical_and(jnp.asarray(t) != 0, jnp.asarray(p) == pairs - 1)

    def from_twin(t, p):
        return jnp.logical_and(jnp.asarray(t) != 0, jnp.asarray(p) < shared)

    def y_arrival(b, p):
        slot = held.at[b, p, side, 1 - w]
        return pltpu.make_async_remote_copy(
            src_ref=slot, dst_ref=slot, send_sem=y_send.at[b, p],
            recv_sem=y_recv.at[b, p], device_id=across_y, device_id_type=MESH,
        )

    def x_copy(b, p, which):
        slot = held.at[b, p, which, 1 - w]
        return pltpu.make_async_remote_copy(
            src_ref=slot, dst_ref=slot, send_sem=x_send.at[b, p],
            recv_sem=x_recv.at[b, p], device_id=across_x, device_id_type=MESH,
        )

    def c_copy(b):
        return pltpu.make_async_remote_copy(
            src_ref=acc.at[b, 1 - core], dst_ref=arrived.at[b], send_sem=c_send.at[b],
            recv_sem=c_recv.at[b], device_id=across_c, device_id_type=MESH,
        )

    @pl.loop(0, pairs)
    def _(p):
        load(p).start()

    barrier = pltpu.get_barrier_semaphore()

    @pl.when(has_left)
    def _():
        pl.semaphore_signal(barrier, inc=1, device_id=left, device_id_type=MESH)

    @pl.when(has_right)
    def _():
        pl.semaphore_signal(barrier, inc=1, device_id=right, device_id_type=MESH)

    for target in (across_y, across_x, across_c):
        pl.semaphore_signal(barrier, inc=1, device_id=target, device_id_type=MESH)
    pl.semaphore_wait(barrier, 3 + has_left.astype(jnp.int32) + has_right.astype(jnp.int32))

    @pl.loop(0, pairs)
    def _(p):
        @pl.when(has_right)
        def _():
            own_z(p, zr_send, right)

        @pl.when(has_left)
        def _():
            own_z(p, zl_send, left)

        y_copy(own_ref.at[p, side], zz, p).start()

    @pl.loop(0, pairs)
    def _(p):
        pltpu.make_async_copy(own_ref.at[p], held.at[zz, p, :, w], own_sem.at[p]).start()

    spread = jnp.broadcast_to(ids_ref[...].astype(jnp.float32), (128, examples)).T
    lanes = lax.broadcasted_iota(jnp.int32, (examples, 128), 1).astype(jnp.float32)
    for tile in range(examples // 128):
        hot[:, tile * 128:(tile + 1) * 128] = jnp.where(
            spread == lanes + float(tile * 128), 1.0, 0.0
        ).astype(jnp.bfloat16)

    @pl.loop(0, pairs)
    def _(p):
        pltpu.make_async_copy(own_ref.at[p], held.at[zz, p, :, w], own_sem.at[p]).wait()

    def both(s, act):
        t = s // pairs
        p = s % pairs
        valid = jnp.logical_and(jnp.asarray(s) >= 0, jnp.asarray(t) < line)

        @pl.when(jnp.logical_and(valid, zz - t >= 0))
        def _():
            act(zz - t, t, p, True)

        @pl.when(jnp.logical_and(jnp.logical_and(valid, jnp.asarray(t) > 0), zz + t < line))
        def _():
            act(zz + t, t, p, False)

    def relay_z(b, t, p, from_left):
        @pl.when(t > 0)
        def _():
            if from_left:
                pass_z(b, p, zr_send, left, landed)

                @pl.when(has_right)
                def _():
                    pass_z(b, p, zr_send, right, begin)
            else:
                pass_z(b, p, zl_send, right, landed)

                @pl.when(has_left)
                def _():
                    pass_z(b, p, zl_send, left, begin)

            @pl.when(p < shared)
            def _():
                twin_copy(b, p, side).start()

            @pl.when(p < pairs - 1)
            def _():
                y_copy(held.at[b, p, side, w], b, p).start()

            @pl.when(p == pairs - 1)
            def _():
                y_whole(b, p, w).start()

    def relay_x(b, t, p, from_left):
        @pl.when(jnp.logical_not(whole_over_y(t, p)))
        def _():
            y_arrival(b, p).wait_recv()
            x_copy(b, p, side).start()

    def multiply(b, t, p, from_left):
        @pl.when(from_twin(t, p))
        def _():
            twin_copy(b, p, 1 - side).wait_recv()

        @pl.when(whole_over_y(t, p))
        def _():
            y_whole(b, p, 1 - w).wait_recv()

        @pl.when(jnp.logical_not(whole_over_y(t, p)))
        def _():
            x_copy(b, p, 1 - side).wait_recv()

        for part in range(2):
            value = None
            for h in range(2):
                term = lax.dot_general(
                    held[b, p, h].reshape(2 * rows, chunk),
                    perm[p, h, part * half:(part + 1) * half, :],
                    (((1,), (1,)), ((), ())), preferred_element_type=jnp.float32,
                )
                value = term if value is None else value + term

            @pl.when(p == 0)
            def _():
                acc[b, part] = value

            @pl.when(p > 0)
            def _():
                acc[b, part] = acc[b, part] + value

        @pl.when(p == pairs - 1)
        def _():
            c_copy(b).start()

    def finish(b, t, p, from_left):
        @pl.when(p == pairs - 1)
        def _():
            c_copy(b).wait_recv()
            out_ref[b] = acc[b, core] + arrived[b]

    @pl.loop(0, pairs)
    def _(p):
        relay_x(zz, 0, p, True)

    def reached(s):
        ready = jnp.minimum(2 * (s - pairs + 1), s + pairs - 1)
        return jnp.minimum(jnp.maximum(ready, 0), line * pairs)

    @pl.loop(0, (line + 1) * pairs)
    def _(s):
        both(s + pairs, relay_z)

        @pl.when(s > 0)
        def _():
            both(s + pairs - 1, relay_x)

        @pl.when(s < pairs)
        def _():
            load(s).wait()

            @pl.loop(0, 4)
            def _(part):
                quarter = examples // 4
                picked = pl.ds(part * quarter, quarter)
                for h in range(2):
                    perm[s, h, picked, :] = jnp.dot(
                        hot[picked, :], stored[s, :, h * chunk:(h + 1) * chunk],
                        preferred_element_type=jnp.float32,
                    ).astype(jnp.bfloat16)

        @pl.loop(reached(s - 1), reached(s))
        def _(m):
            both(m, multiply)
            both(m - 1, finish)

    both(line * pairs - 1, finish)

    @pl.loop(0, line * pairs)
    def _(s):
        b = s // pairs
        p = s % pairs

        @pl.when(jnp.logical_and(has_right, b <= zz))
        def _():
            pass_z(b, p, zr_send, right, left_here)

        @pl.when(jnp.logical_and(has_left, b >= zz))
        def _():
            pass_z(b, p, zl_send, left, left_here)

        t = b - zz

        @pl.when(from_twin(t, p))
        def _():
            twin_copy(b, p, side).wait_send()

        @pl.when(whole_over_y(t, p))
        def _():
            y_whole(b, p, w).wait_send()

        @pl.when(jnp.logical_not(whole_over_y(t, p)))
        def _():
            y_copy(held.at[b, p, side, w], b, p).wait_send()
            x_copy(b, p, side).wait_send()

        @pl.when(p == 0)
        def _():
            c_copy(b).wait_send()


def scores_of(own, ids, train, devices):
    rows = own.shape[2]
    chunk = own.shape[3]
    examples = train.shape[0]
    line = devices // 2
    dma = pltpu.SemaphoreType.DMA
    grid_sems = [dma((line, pairs)) for _ in range(9)]
    return pl.pallas_call(
        functools.partial(score_kernel, line),
        out_shape=jax.ShapeDtypeStruct((line, 2 * rows, examples // 2), jnp.float32),
        in_specs=[
            pl.BlockSpec(memory_space=pltpu.VMEM),
            pl.BlockSpec(memory_space=pltpu.VMEM),
            pl.BlockSpec(memory_space=pl.ANY),
        ],
        out_specs=pl.BlockSpec(memory_space=pltpu.VMEM),
        scratch_shapes=[
            pltpu.VMEM((pairs, examples, 2 * chunk), jnp.bfloat16),
            pltpu.VMEM((examples, examples), jnp.bfloat16),
            pltpu.VMEM((pairs, 2, examples, chunk), jnp.bfloat16),
            pltpu.VMEM((line, pairs, 2, 2, rows, chunk), jnp.bfloat16),
            pltpu.VMEM((line, 2, 2 * rows, examples // 2), jnp.float32),
            pltpu.VMEM((line, 2 * rows, examples // 2), jnp.float32),
            dma((pairs,)),
            dma((pairs,)),
            *grid_sems,
            dma((line,)),
            dma((line,)),
        ],
        compiler_params=pltpu.CompilerParams(
            collective_id=0, has_side_effects=True, vmem_limit_bytes=56 * 1024 * 1024
        ),
    )(own, ids, train)


def shards(devices, queries, basis_s, basis_a, eigvals, train_grads, example_ids):
    stored = train_grads.reshape(train_grads.shape[0], -1)
    own_rows = precondition(queries, basis_s, basis_a, eigvals)
    rows = own_rows.shape[0]
    cut = own_rows.reshape(rows, 2 * pairs, -1).transpose(1, 0, 2)
    cut = cut.reshape(pairs, 2, rows, cut.shape[-1])
    scores = scores_of(cut, example_ids, stored, devices)
    return scores.reshape(devices * rows, -1)


def solution(mesh):
    return jax.shard_map(
        functools.partial(shards, mesh.shape["ex"]),
        mesh=mesh,
        in_specs=(
            P("ex", "lay", None),
            P("lay", None, None),
            P("lay", None, None),
            P("lay", None, None),
            P(("grp", "ex"), "lay", None),
            P(("grp", "ex"), None),
        ),
        out_specs=P(None, ("grp", "ex", "lay")),
        check_vma=False,
    )
```

```python
import functools

import jax
import jax.numpy as jnp
from jax import lax
from jax.experimental import pallas as pl
from jax.experimental.pallas import tpu as pltpu
from jax.sharding import PartitionSpec as P

damp_ratio = 0.1
pairs = 4
shared = 2
MESH = pl.DeviceIdType.MESH


def precondition(grads, basis_s, basis_a, eigvals):
    number_rows = grads.shape[0]
    layer_count = grads.shape[1]
    rank = basis_s.shape[-1]
    highest = lax.Precision.HIGHEST
    expanded = grads.astype(jnp.float32).reshape(number_rows, layer_count, rank, rank)
    half_turn = jnp.einsum("nlik,lkm->nlim", expanded, basis_a, precision=highest)
    rotated = jnp.einsum("lij,nlim->nljm", basis_s, half_turn, precision=highest)
    damping = damp_ratio * jnp.mean(eigvals, axis=(1, 2), keepdims=True)
    scaled = rotated / (eigvals + damping)[None]
    turned_back = jnp.einsum("nljm,lpm->nljp", scaled, basis_a, precision=highest)
    restored = jnp.einsum("lij,nljp->nlip", basis_s, turned_back, precision=highest)
    return restored.reshape(number_rows, layer_count, rank * rank).astype(jnp.bfloat16)


def score_kernel(
    line, own_ref, ids_ref, train_ref, out_ref,
    stored, hot, held, acc, arrived,
    load_sem, own_sem, z_recv, zr_send, zl_send, y_recv, y_send, x_recv, x_send, twin_recv, twin_send,
    c_recv, c_send,
):
    grp = lax.axis_index("grp")
    ex = lax.axis_index("ex")
    core = lax.axis_index("lay")
    zz = ex // 2
    w = ex % 2
    side = grp % 2
    rows = own_ref.shape[2]
    examples = train_ref.shape[0]
    chunk = own_ref.shape[3]
    half = examples // 2
    right = {"ex": lax.rem(ex + 2, 2 * line)}
    left = {"ex": lax.rem(ex + 2 * line - 2, 2 * line)}
    across_y = {"ex": zz * 2 + (1 - w)}
    across_x = {"grp": (grp // 2) * 2 + (1 - side)}
    across_c = {"lay": 1 - core}
    has_left = zz > 0
    has_right = zz < line - 1

    def load(p):
        return pltpu.make_async_copy(
            train_ref.at[:, pl.ds(p * 2 * chunk, 2 * chunk)], stored.at[p], load_sem.at[p]
        )

    def pick(p, first, second):
        @pl.when(p < shared)
        def _():
            first()

        @pl.when(p >= shared)
        def _():
            second()

    def z_copy(src, b, p, which, send, target):
        return pltpu.make_async_remote_copy(
            src_ref=src, dst_ref=held.at[b, p, which, w], send_sem=send.at[b, p],
            recv_sem=z_recv.at[b, p], device_id=target, device_id_type=MESH,
        )

    def own_z(p, send, target):
        pick(
            p,
            lambda: z_copy(own_ref.at[p, side], zz, p, side, send, target).start(),
            lambda: z_copy(own_ref.at[p], zz, p, slice(None), send, target).start(),
        )

    def pass_z(b, p, send, target, act):
        pick(
            p,
            lambda: act(z_copy(held.at[b, p, side, w], b, p, side, send, target)),
            lambda: act(z_copy(held.at[b, p, :, w], b, p, slice(None), send, target)),
        )

    def begin(copy):
        copy.start()

    def landed(copy):
        copy.wait_recv()

    def left_here(copy):
        copy.wait_send()

    def y_copy(src, b, p):
        return pltpu.make_async_remote_copy(
            src_ref=src, dst_ref=held.at[b, p, side, w], send_sem=y_send.at[b, p],
            recv_sem=y_recv.at[b, p], device_id=across_y, device_id_type=MESH,
        )

    def y_whole(b, p, column):
        slot = held.at[b, p, :, column]
        return pltpu.make_async_remote_copy(
            src_ref=slot, dst_ref=slot, send_sem=y_send.at[b, p],
            recv_sem=y_recv.at[b, p], device_id=across_y, device_id_type=MESH,
        )

    def twin_copy(b, p, which):
        slot = held.at[b, p, which, w]
        return pltpu.make_async_remote_copy(
            src_ref=slot, dst_ref=slot, send_sem=twin_send.at[b, p],
            recv_sem=twin_recv.at[b, p], device_id=across_x, device_id_type=MESH,
        )

    def whole_over_y(t, p):
        return jnp.logical_and(jnp.asarray(t) != 0, jnp.asarray(p) == pairs - 1)

    def from_twin(t, p):
        return jnp.logical_and(jnp.asarray(t) != 0, jnp.asarray(p) < shared)

    def y_arrival(b, p):
        slot = held.at[b, p, side, 1 - w]
        return pltpu.make_async_remote_copy(
            src_ref=slot, dst_ref=slot, send_sem=y_send.at[b, p],
            recv_sem=y_recv.at[b, p], device_id=across_y, device_id_type=MESH,
        )

    def x_copy(b, p, which):
        slot = held.at[b, p, which, 1 - w]
        return pltpu.make_async_remote_copy(
            src_ref=slot, dst_ref=slot, send_sem=x_send.at[b, p],
            recv_sem=x_recv.at[b, p], device_id=across_x, device_id_type=MESH,
        )

    def c_copy(b):
        return pltpu.make_async_remote_copy(
            src_ref=acc.at[b, 1 - core], dst_ref=arrived.at[b], send_sem=c_send.at[b],
            recv_sem=c_recv.at[b], device_id=across_c, device_id_type=MESH,
        )

    @pl.loop(0, pairs)
    def _(p):
        load(p).start()

    barrier = pltpu.get_barrier_semaphore()

    @pl.when(has_left)
    def _():
        pl.semaphore_signal(barrier, inc=1, device_id=left, device_id_type=MESH)

    @pl.when(has_right)
    def _():
        pl.semaphore_signal(barrier, inc=1, device_id=right, device_id_type=MESH)

    for target in (across_y, across_x, across_c):
        pl.semaphore_signal(barrier, inc=1, device_id=target, device_id_type=MESH)
    pl.semaphore_wait(barrier, 3 + has_left.astype(jnp.int32) + has_right.astype(jnp.int32))

    @pl.loop(0, pairs)
    def _(p):
        @pl.when(has_right)
        def _():
            own_z(p, zr_send, right)

        @pl.when(has_left)
        def _():
            own_z(p, zl_send, left)

        y_copy(own_ref.at[p, side], zz, p).start()

    @pl.loop(0, pairs)
    def _(p):
        pltpu.make_async_copy(own_ref.at[p], held.at[zz, p, :, w], own_sem.at[p]).start()

    spread = jnp.broadcast_to(ids_ref[...].astype(jnp.float32), (128, examples)).T
    lanes = lax.broadcasted_iota(jnp.int32, (examples, 128), 1).astype(jnp.float32)
    for tile in range(examples // 128):
        hot[:, tile * 128:(tile + 1) * 128] = jnp.where(
            spread == lanes + float(tile * 128), 1.0, 0.0
        ).astype(jnp.bfloat16)

    @pl.loop(0, pairs)
    def _(p):
        pltpu.make_async_copy(own_ref.at[p], held.at[zz, p, :, w], own_sem.at[p]).wait()

    def both(s, act):
        t = s // pairs
        p = s % pairs
        valid = jnp.logical_and(jnp.asarray(s) >= 0, jnp.asarray(t) < line)

        @pl.when(jnp.logical_and(valid, zz - t >= 0))
        def _():
            act(zz - t, t, p, True)

        @pl.when(jnp.logical_and(jnp.logical_and(valid, jnp.asarray(t) > 0), zz + t < line))
        def _():
            act(zz + t, t, p, False)

    def relay_z(b, t, p, from_left):
        @pl.when(t > 0)
        def _():
            if from_left:
                pass_z(b, p, zr_send, left, landed)

                @pl.when(has_right)
                def _():
                    pass_z(b, p, zr_send, right, begin)
            else:
                pass_z(b, p, zl_send, right, landed)

                @pl.when(has_left)
                def _():
                    pass_z(b, p, zl_send, left, begin)

            @pl.when(p < shared)
            def _():
                twin_copy(b, p, side).start()

            @pl.when(p < pairs - 1)
            def _():
                y_copy(held.at[b, p, side, w], b, p).start()

            @pl.when(p == pairs - 1)
            def _():
                y_whole(b, p, w).start()

    def relay_x(b, t, p, from_left):
        @pl.when(jnp.logical_not(whole_over_y(t, p)))
        def _():
            y_arrival(b, p).wait_recv()
            x_copy(b, p, side).start()

    def reorder(b):
        pieces = []
        for source in range(2):
            rest = acc[b, source]
            terms = []
            for _ in range(3):
                term = rest.astype(jnp.bfloat16)
                terms.append(term)
                rest = rest - term.astype(jnp.float32)
            pieces.append(jnp.concatenate(terms, axis=0))
        ordered = []
        for part in range(2):
            value = None
            for source in range(2):
                term = lax.dot_general(
                    pieces[source],
                    hot[part * half:(part + 1) * half, source * half:(source + 1) * half],
                    (((1,), (1,)), ((), ())), preferred_element_type=jnp.float32,
                )
                value = term if value is None else value + term
            block = 2 * rows
            ordered.append(value[:block] + value[block:2 * block] + value[2 * block:])
        for part in range(2):
            acc[b, part] = ordered[part]

    def multiply(b, t, p, from_left):
        @pl.when(t == 0)
        def _():
            load(p).wait()

        @pl.when(from_twin(t, p))
        def _():
            twin_copy(b, p, 1 - side).wait_recv()

        @pl.when(whole_over_y(t, p))
        def _():
            y_whole(b, p, 1 - w).wait_recv()

        @pl.when(jnp.logical_not(whole_over_y(t, p)))
        def _():
            x_copy(b, p, 1 - side).wait_recv()

        for part in range(2):
            value = None
            for h in range(2):
                term = lax.dot_general(
                    held[b, p, h].reshape(2 * rows, chunk),
                    stored[p, part * half:(part + 1) * half, h * chunk:(h + 1) * chunk],
                    (((1,), (1,)), ((), ())), preferred_element_type=jnp.float32,
                )
                value = term if value is None else value + term

            @pl.when(p == 0)
            def _():
                acc[b, part] = value

            @pl.when(p > 0)
            def _():
                acc[b, part] = acc[b, part] + value

        @pl.when(p == pairs - 1)
        def _():
            reorder(b)
            c_copy(b).start()

    def finish(b, t, p, from_left):
        @pl.when(p == pairs - 1)
        def _():
            c_copy(b).wait_recv()
            out_ref[b] = acc[b, core] + arrived[b]

    @pl.loop(0, pairs)
    def _(p):
        relay_x(zz, 0, p, True)

    def reached(s):
        ready = jnp.minimum(3 * jnp.maximum(s, 0) // 2, s + pairs - 1)
        return jnp.minimum(jnp.maximum(ready, 0), line * pairs)

    @pl.loop(0, (line + 1) * pairs)
    def _(s):
        both(s + pairs, relay_z)

        @pl.when(s > 0)
        def _():
            both(s + pairs - 1, relay_x)

        @pl.loop(reached(s - 1), reached(s))
        def _(m):
            both(m, multiply)
            both(m - 1, finish)

    both(line * pairs - 1, finish)

    @pl.loop(0, line * pairs)
    def _(s):
        b = s // pairs
        p = s % pairs

        @pl.when(jnp.logical_and(has_right, b <= zz))
        def _():
            pass_z(b, p, zr_send, right, left_here)

        @pl.when(jnp.logical_and(has_left, b >= zz))
        def _():
            pass_z(b, p, zl_send, left, left_here)

        t = b - zz

        @pl.when(from_twin(t, p))
        def _():
            twin_copy(b, p, side).wait_send()

        @pl.when(whole_over_y(t, p))
        def _():
            y_whole(b, p, w).wait_send()

        @pl.when(jnp.logical_not(whole_over_y(t, p)))
        def _():
            y_copy(held.at[b, p, side, w], b, p).wait_send()
            x_copy(b, p, side).wait_send()

        @pl.when(p == 0)
        def _():
            c_copy(b).wait_send()


def scores_of(own, ids, train, devices):
    rows = own.shape[2]
    chunk = own.shape[3]
    examples = train.shape[0]
    line = devices // 2
    dma = pltpu.SemaphoreType.DMA
    grid_sems = [dma((line, pairs)) for _ in range(9)]
    return pl.pallas_call(
        functools.partial(score_kernel, line),
        out_shape=jax.ShapeDtypeStruct((line, 2 * rows, examples // 2), jnp.float32),
        in_specs=[
            pl.BlockSpec(memory_space=pltpu.VMEM),
            pl.BlockSpec(memory_space=pltpu.VMEM),
            pl.BlockSpec(memory_space=pl.ANY),
        ],
        out_specs=pl.BlockSpec(memory_space=pltpu.VMEM),
        scratch_shapes=[
            pltpu.VMEM((pairs, examples, 2 * chunk), jnp.bfloat16),
            pltpu.VMEM((examples, examples), jnp.bfloat16),
            pltpu.VMEM((line, pairs, 2, 2, rows, chunk), jnp.bfloat16),
            pltpu.VMEM((line, 2, 2 * rows, examples // 2), jnp.float32),
            pltpu.VMEM((line, 2 * rows, examples // 2), jnp.float32),
            dma((pairs,)),
            dma((pairs,)),
            *grid_sems,
            dma((line,)),
            dma((line,)),
        ],
        compiler_params=pltpu.CompilerParams(
            collective_id=0, has_side_effects=True, vmem_limit_bytes=56 * 1024 * 1024
        ),
    )(own, ids, train)


def shards(devices, queries, basis_s, basis_a, eigvals, train_grads, example_ids):
    stored = train_grads.reshape(train_grads.shape[0], -1)
    own_rows = precondition(queries, basis_s, basis_a, eigvals)
    rows = own_rows.shape[0]
    cut = own_rows.reshape(rows, 2 * pairs, -1).transpose(1, 0, 2)
    cut = cut.reshape(pairs, 2, rows, cut.shape[-1])
    scores = scores_of(cut, example_ids, stored, devices)
    return scores.reshape(devices * rows, -1)


def solution(mesh):
    return jax.shard_map(
        functools.partial(shards, mesh.shape["ex"]),
        mesh=mesh,
        in_specs=(
            P("ex", "lay", None),
            P("lay", None, None),
            P("lay", None, None),
            P("lay", None, None),
            P(("grp", "ex"), "lay", None),
            P(("grp", "ex"), None),
        ),
        out_specs=P(None, ("grp", "ex", "lay")),
        check_vma=False,
    )
```

```python
import functools

import jax
import jax.numpy as jnp
from jax import lax
from jax.experimental import pallas as pl
from jax.experimental.pallas import tpu as pltpu
from jax.sharding import PartitionSpec as P

damp_ratio = 0.1
pairs = 4
shared = 2
MESH = pl.DeviceIdType.MESH


def precondition(grads, basis_s, basis_a, eigvals):
    number_rows = grads.shape[0]
    layer_count = grads.shape[1]
    rank = basis_s.shape[-1]
    high = lax.Precision.HIGH
    expanded = grads.astype(jnp.float32).reshape(number_rows, layer_count, rank, rank)
    half_turn = jnp.einsum("nlik,lkm->nlim", expanded, basis_a, precision=high)
    rotated = jnp.einsum("lij,nlim->nljm", basis_s, half_turn, precision=high)
    damping = damp_ratio * jnp.mean(eigvals, axis=(1, 2), keepdims=True)
    scaled = rotated / (eigvals + damping)[None]
    turned_back = jnp.einsum("nljm,lpm->nljp", scaled, basis_a, precision=high)
    restored = jnp.einsum("lij,nljp->nlip", basis_s, turned_back, precision=high)
    return restored.reshape(number_rows, layer_count, rank * rank).astype(jnp.bfloat16)


def score_kernel(
    line, own_ref, ids_ref, train_ref, out_ref,
    stored, hot, perm, held, acc, arrived,
    load_sem, own_sem, z_recv, zr_send, zl_send, y_recv, y_send, x_recv, x_send, twin_recv, twin_send,
    c_recv, c_send,
):
    grp = lax.axis_index("grp")
    ex = lax.axis_index("ex")
    core = lax.axis_index("lay")
    zz = ex // 2
    w = ex % 2
    side = grp % 2
    rows = own_ref.shape[2]
    examples = train_ref.shape[0]
    chunk = own_ref.shape[3]
    half = examples // 2
    right = {"ex": lax.rem(ex + 2, 2 * line)}
    left = {"ex": lax.rem(ex + 2 * line - 2, 2 * line)}
    across_y = {"ex": zz * 2 + (1 - w)}
    across_x = {"grp": (grp // 2) * 2 + (1 - side)}
    across_c = {"lay": 1 - core}
    has_left = zz > 0
    has_right = zz < line - 1

    def load(p):
        return pltpu.make_async_copy(
            train_ref.at[:, pl.ds(p * 2 * chunk, 2 * chunk)], stored.at[p], load_sem.at[p]
        )

    def pick(p, first, second):
        @pl.when(p < shared)
        def _():
            first()

        @pl.when(p >= shared)
        def _():
            second()

    def z_copy(src, b, p, which, send, target):
        return pltpu.make_async_remote_copy(
            src_ref=src, dst_ref=held.at[b, p, which, w], send_sem=send.at[b, p],
            recv_sem=z_recv.at[b, p], device_id=target, device_id_type=MESH,
        )

    def own_z(p, send, target):
        pick(
            p,
            lambda: z_copy(own_ref.at[p, side], zz, p, side, send, target).start(),
            lambda: z_copy(own_ref.at[p], zz, p, slice(None), send, target).start(),
        )

    def pass_z(b, p, send, target, act):
        pick(
            p,
            lambda: act(z_copy(held.at[b, p, side, w], b, p, side, send, target)),
            lambda: act(z_copy(held.at[b, p, :, w], b, p, slice(None), send, target)),
        )

    def begin(copy):
        copy.start()

    def landed(copy):
        copy.wait_recv()

    def left_here(copy):
        copy.wait_send()

    def y_copy(src, b, p):
        return pltpu.make_async_remote_copy(
            src_ref=src, dst_ref=held.at[b, p, side, w], send_sem=y_send.at[b, p],
            recv_sem=y_recv.at[b, p], device_id=across_y, device_id_type=MESH,
        )

    def y_whole(b, p, column):
        slot = held.at[b, p, :, column]
        return pltpu.make_async_remote_copy(
            src_ref=slot, dst_ref=slot, send_sem=y_send.at[b, p],
            recv_sem=y_recv.at[b, p], device_id=across_y, device_id_type=MESH,
        )

    def twin_copy(b, p, which):
        slot = held.at[b, p, which, w]
        return pltpu.make_async_remote_copy(
            src_ref=slot, dst_ref=slot, send_sem=twin_send.at[b, p],
            recv_sem=twin_recv.at[b, p], device_id=across_x, device_id_type=MESH,
        )

    def whole_over_y(t, p):
        return jnp.logical_and(jnp.asarray(t) != 0, jnp.asarray(p) == pairs - 1)

    def from_twin(t, p):
        return jnp.logical_and(jnp.asarray(t) != 0, jnp.asarray(p) < shared)

    def y_arrival(b, p):
        slot = held.at[b, p, side, 1 - w]
        return pltpu.make_async_remote_copy(
            src_ref=slot, dst_ref=slot, send_sem=y_send.at[b, p],
            recv_sem=y_recv.at[b, p], device_id=across_y, device_id_type=MESH,
        )

    def x_copy(b, p, which):
        slot = held.at[b, p, which, 1 - w]
        return pltpu.make_async_remote_copy(
            src_ref=slot, dst_ref=slot, send_sem=x_send.at[b, p],
            recv_sem=x_recv.at[b, p], device_id=across_x, device_id_type=MESH,
        )

    def c_copy(b):
        return pltpu.make_async_remote_copy(
            src_ref=acc.at[b, 1 - core], dst_ref=arrived.at[b], send_sem=c_send.at[b],
            recv_sem=c_recv.at[b], device_id=across_c, device_id_type=MESH,
        )

    @pl.loop(0, pairs)
    def _(p):
        load(p).start()

    barrier = pltpu.get_barrier_semaphore()

    @pl.when(has_left)
    def _():
        pl.semaphore_signal(barrier, inc=1, device_id=left, device_id_type=MESH)

    @pl.when(has_right)
    def _():
        pl.semaphore_signal(barrier, inc=1, device_id=right, device_id_type=MESH)

    for target in (across_y, across_x, across_c):
        pl.semaphore_signal(barrier, inc=1, device_id=target, device_id_type=MESH)
    pl.semaphore_wait(barrier, 3 + has_left.astype(jnp.int32) + has_right.astype(jnp.int32))

    @pl.loop(0, pairs)
    def _(p):
        @pl.when(has_right)
        def _():
            own_z(p, zr_send, right)

        @pl.when(has_left)
        def _():
            own_z(p, zl_send, left)

        y_copy(own_ref.at[p, side], zz, p).start()

    @pl.loop(0, pairs)
    def _(p):
        pltpu.make_async_copy(own_ref.at[p], held.at[zz, p, :, w], own_sem.at[p]).start()

    spread = jnp.broadcast_to(ids_ref[...].astype(jnp.float32), (128, examples)).T
    lanes = lax.broadcasted_iota(jnp.int32, (examples, 128), 1).astype(jnp.float32)
    for tile in range(examples // 128):
        hot[:, tile * 128:(tile + 1) * 128] = jnp.where(
            spread == lanes + float(tile * 128), 1.0, 0.0
        ).astype(jnp.bfloat16)

    @pl.loop(0, pairs)
    def _(p):
        pltpu.make_async_copy(own_ref.at[p], held.at[zz, p, :, w], own_sem.at[p]).wait()

    def both(s, act):
        t = s // pairs
        p = s % pairs
        valid = jnp.logical_and(jnp.asarray(s) >= 0, jnp.asarray(t) < line)

        @pl.when(jnp.logical_and(valid, zz - t >= 0))
        def _():
            act(zz - t, t, p, True)

        @pl.when(jnp.logical_and(jnp.logical_and(valid, jnp.asarray(t) > 0), zz + t < line))
        def _():
            act(zz + t, t, p, False)

    def relay_z(b, t, p, from_left):
        @pl.when(t > 0)
        def _():
            if from_left:
                pass_z(b, p, zr_send, left, landed)

                @pl.when(has_right)
                def _():
                    pass_z(b, p, zr_send, right, begin)
            else:
                pass_z(b, p, zl_send, right, landed)

                @pl.when(has_left)
                def _():
                    pass_z(b, p, zl_send, left, begin)

            @pl.when(p < shared)
            def _():
                twin_copy(b, p, side).start()

            @pl.when(p < pairs - 1)
            def _():
                y_copy(held.at[b, p, side, w], b, p).start()

            @pl.when(p == pairs - 1)
            def _():
                y_whole(b, p, w).start()

    def relay_x(b, t, p, from_left):
        @pl.when(jnp.logical_not(whole_over_y(t, p)))
        def _():
            y_arrival(b, p).wait_recv()
            x_copy(b, p, side).start()

    def multiply(b, t, p, from_left):
        @pl.when(from_twin(t, p))
        def _():
            twin_copy(b, p, 1 - side).wait_recv()

        @pl.when(whole_over_y(t, p))
        def _():
            y_whole(b, p, 1 - w).wait_recv()

        @pl.when(jnp.logical_not(whole_over_y(t, p)))
        def _():
            x_copy(b, p, 1 - side).wait_recv()

        for part in range(2):
            value = None
            for h in range(2):
                term = lax.dot_general(
                    held[b, p, h].reshape(2 * rows, chunk),
                    perm[p, h, part * half:(part + 1) * half, :],
                    (((1,), (1,)), ((), ())), preferred_element_type=jnp.float32,
                )
                value = term if value is None else value + term

            @pl.when(p == 0)
            def _():
                acc[b, part] = value

            @pl.when(p > 0)
            def _():
                acc[b, part] = acc[b, part] + value

        @pl.when(p == pairs - 1)
        def _():
            c_copy(b).start()

    def finish(b, t, p, from_left):
        @pl.when(p == pairs - 1)
        def _():
            c_copy(b).wait_recv()
            out_ref[b] = acc[b, core] + arrived[b]

    @pl.loop(0, pairs)
    def _(p):
        relay_x(zz, 0, p, True)

    def reached(s):
        ready = jnp.minimum(2 * (s - pairs + 1), s + pairs - 1)
        return jnp.minimum(jnp.maximum(ready, 0), line * pairs)

    @pl.loop(0, (line + 1) * pairs)
    def _(s):
        both(s + pairs, relay_z)

        @pl.when(s > 0)
        def _():
            both(s + pairs - 1, relay_x)

        @pl.when(s < pairs)
        def _():
            load(s).wait()

            @pl.loop(0, 4)
            def _(part):
                quarter = examples // 4
                picked = pl.ds(part * quarter, quarter)
                for h in range(2):
                    perm[s, h, picked, :] = jnp.dot(
                        hot[picked, :], stored[s, :, h * chunk:(h + 1) * chunk],
                        preferred_element_type=jnp.float32,
                    ).astype(jnp.bfloat16)

        @pl.loop(reached(s - 1), reached(s))
        def _(m):
            both(m, multiply)
            both(m - 1, finish)

    both(line * pairs - 1, finish)

    @pl.loop(0, line * pairs)
    def _(s):
        b = s // pairs
        p = s % pairs

        @pl.when(jnp.logical_and(has_right, b <= zz))
        def _():
            pass_z(b, p, zr_send, right, left_here)

        @pl.when(jnp.logical_and(has_left, b >= zz))
        def _():
            pass_z(b, p, zl_send, left, left_here)

        t = b - zz

        @pl.when(from_twin(t, p))
        def _():
            twin_copy(b, p, side).wait_send()

        @pl.when(whole_over_y(t, p))
        def _():
            y_whole(b, p, w).wait_send()

        @pl.when(jnp.logical_not(whole_over_y(t, p)))
        def _():
            y_copy(held.at[b, p, side, w], b, p).wait_send()
            x_copy(b, p, side).wait_send()

        @pl.when(p == 0)
        def _():
            c_copy(b).wait_send()


def scores_of(own, ids, train, devices):
    rows = own.shape[2]
    chunk = own.shape[3]
    examples = train.shape[0]
    line = devices // 2
    dma = pltpu.SemaphoreType.DMA
    grid_sems = [dma((line, pairs)) for _ in range(9)]
    return pl.pallas_call(
        functools.partial(score_kernel, line),
        out_shape=jax.ShapeDtypeStruct((line, 2 * rows, examples // 2), jnp.float32),
        in_specs=[
            pl.BlockSpec(memory_space=pltpu.VMEM),
            pl.BlockSpec(memory_space=pltpu.VMEM),
            pl.BlockSpec(memory_space=pl.ANY),
        ],
        out_specs=pl.BlockSpec(memory_space=pltpu.VMEM),
        scratch_shapes=[
            pltpu.VMEM((pairs, examples, 2 * chunk), jnp.bfloat16),
            pltpu.VMEM((examples, examples), jnp.bfloat16),
            pltpu.VMEM((pairs, 2, examples, chunk), jnp.bfloat16),
            pltpu.VMEM((line, pairs, 2, 2, rows, chunk), jnp.bfloat16),
            pltpu.VMEM((line, 2, 2 * rows, examples // 2), jnp.float32),
            pltpu.VMEM((line, 2 * rows, examples // 2), jnp.float32),
            dma((pairs,)),
            dma((pairs,)),
            *grid_sems,
            dma((line,)),
            dma((line,)),
        ],
        compiler_params=pltpu.CompilerParams(
            collective_id=0, has_side_effects=True, vmem_limit_bytes=56 * 1024 * 1024
        ),
    )(own, ids, train)


def shards(devices, queries, basis_s, basis_a, eigvals, train_grads, example_ids):
    stored = train_grads.reshape(train_grads.shape[0], -1)
    own_rows = precondition(queries, basis_s, basis_a, eigvals)
    rows = own_rows.shape[0]
    cut = own_rows.reshape(rows, 2 * pairs, -1).transpose(1, 0, 2)
    cut = cut.reshape(pairs, 2, rows, cut.shape[-1])
    scores = scores_of(cut, example_ids, stored, devices)
    return scores.reshape(devices * rows, -1)


def solution(mesh):
    return jax.shard_map(
        functools.partial(shards, mesh.shape["ex"]),
        mesh=mesh,
        in_specs=(
            P("ex", "lay", None),
            P("lay", None, None),
            P("lay", None, None),
            P("lay", None, None),
            P(("grp", "ex"), "lay", None),
            P(("grp", "ex"), None),
        ),
        out_specs=P(None, ("grp", "ex", "lay")),
        check_vma=False,
    )
```
